256 devices in a mesh: row: 32 (over x_hi, z, core), col: 8 (over y, x_lo).
Axes of the slice: x: 4 (x_hi: 2, x_lo: 2; x = x_hi * 2 + x_lo), y: 4, z: 8, core: 2. Of those that a mesh axis runs over, the one named last changes fastest.
Arguments:
- object_field: float32 [2, 2, 8192, 2048], P(None, None, 'row', 'col'), may hold values from -4 to 4
- probe_wave: float32 [2, 256, 256], replicated, may hold values from -6 to 6
- positions: int32 [32, 8, 6, 2], P('row', 'col'), may hold values from 0 to 256, as said below
- counts: int32 [32, 8], P('row', 'col'), may hold values from 1 to 6, as said below
- amplitudes: bfloat16 [32, 8, 6, 256, 256], P('row', 'col'), may hold values from 0 to 3
Outputs:
- updated_object: float32 [2, 2, 8192, 2048], P(None, None, 'row', 'col')
The draws below stay inside these ranges and needn't reach their ends.
Inputs may be any that keep to these rules, and one draw needn't show every extreme that they name: `positions`: the window of a slot covers 256 x 256 pixels of a frame that begins 128 pixels above and left of its tile. Slots at and after the tile's count are unused. `counts`: some tile uses all 6 slots in every draw.
All inputs are finite; a program needn't handle non-finite values.
Results may differ from the reference program's by a relative error of at most 0.024.
Values may be sent and summed in bfloat16 or wider, within the bound.
No kernel may reach another device: no remote copies, remote signals or barrier semaphores. Data moves between devices by JAX's collectives and lax.ppermute only.
A program may use at most 64 MiB of HBM per device.

```python
import jax
import jax.numpy as jnp
from jax import lax

PROBE = 256
TILE = 256
P_MAX = 6
ITERS = 2
NY = 8192
NX = 2048
N_ROW = 32
N_COL = 8


def draw_positions(key, part):
    subkeys = jax.random.split(jax.random.fold_in(key, 11), 3)
    entries = N_ROW * N_COL * P_MAX * 2
    flattened = jax.random.randint(subkeys[0], (entries,), 0, TILE + 1, dtype=jnp.int32)
    low_at = jax.random.randint(subkeys[1], (), 0, entries, dtype=jnp.int32)
    high_at = (low_at + 1 + jax.random.randint(subkeys[2], (), 0, entries - 1, dtype=jnp.int32)) % entries
    flattened = flattened.at[low_at].set(0).at[high_at].set(TILE)
    return flattened.reshape(N_ROW, N_COL, P_MAX, 2).astype(jnp.int32)


def draw_counts(key, part):
    subkeys = jax.random.split(jax.random.fold_in(key, 23), 3)
    baseline = jax.random.randint(subkeys[0], (N_ROW, N_COL), 1, 3, dtype=jnp.int32)
    crowded = jax.random.randint(subkeys[1], (N_ROW, N_COL), 0, 8, dtype=jnp.int32) == 0
    filled = jnp.where(crowded, P_MAX, baseline)
    chosen = jax.random.randint(subkeys[2], (), 0, N_ROW * N_COL, dtype=jnp.int32)
    flattened = filled.reshape(-1).at[chosen].set(P_MAX)
    return flattened.reshape(N_ROW, N_COL).astype(jnp.int32)


def block_scale(key, shape, cuts, low, largest):
    loudness, own = 1.0, jax.random.fold_in(key, 6)
    for position, parts in cuts:
        draws = jnp.exp(jax.random.uniform(jax.random.fold_in(own, position), (parts,), jnp.float32, low / len(cuts), largest / len(cuts)))
        loudness = loudness * jnp.repeat(draws, shape[position] // parts).reshape([-1 if axis == position else 1 for axis in range(len(shape))])
    return loudness


def bell_draw(stream_key, shape, scale, bound, pieces=(), kind=jnp.bfloat16):
    array = jax.random.normal(stream_key, shape, jnp.float32) * scale
    if len(pieces) > 0:
        array = block_scale(stream_key, shape, pieces, -0.22, 0.18) * array
    return jnp.clip(array, min=-bound, max=bound).astype(kind)


def setup_inputs(seed: int = 0) -> dict:
    seeds = jax.random.split(jax.random.key(seed), 6)
    object_field = bell_draw(seeds[0], (2, 2, NY, NX), 0.5, 4.0, ((2, 32), (3, 8)), jnp.float32)
    probe_wave = bell_draw(seeds[1], (2, PROBE, PROBE), 1.0, 6.0, (), jnp.float32)
    positions = draw_positions(jax.random.fold_in(seeds[5], 71), 0)
    counts = draw_counts(jax.random.fold_in(seeds[5], 71), 0)
    amplitudes = jnp.clip(3.0 * jax.random.uniform(seeds[4], (N_ROW, N_COL, P_MAX, PROBE, PROBE), jnp.float32) ** block_scale(seeds[4], (N_ROW, N_COL, P_MAX, PROBE, PROBE), ((0, 32), (1, 8)), -0.2, 0.2), 0.0, 3.0).astype(jnp.bfloat16)
    return {"object_field": object_field, "probe_wave": probe_wave, "positions": positions, "counts": counts, "amplitudes": amplitudes}


smooth_floor = 0.25
descent_rate = 0.1

def make_tables(points):
    indices = jnp.arange(points, dtype=jnp.int32)
    products = indices[:, None] * indices[None, :] % points
    phases = 2.0 * jnp.pi / points * products.astype(jnp.float32)
    scaling = 1.0 / jnp.sqrt(jnp.float32(points))
    cosines = jnp.cos(phases)
    sine_table = jnp.sin(phases)
    fourier = ((cosines * scaling).astype(jnp.bfloat16), (-sine_table * scaling).astype(jnp.bfloat16))
    frequency = jnp.where(indices < points // 2, indices, indices - points).astype(jnp.float32)
    chirp_phase = -jnp.pi / (2.0 * points) * frequency * frequency
    chirp_cos = jnp.cos(chirp_phase)[None, :]
    chirp_sin = jnp.sin(chirp_phase)[None, :]
    highest = lax.Precision.HIGHEST
    cos_real = jnp.dot(cosines * chirp_cos, cosines, precision=highest)
    sin_real = jnp.dot(sine_table * chirp_cos, sine_table, precision=highest)
    sin_imag = jnp.dot(sine_table * chirp_sin, cosines, precision=highest)
    cos_imag = jnp.dot(cosines * chirp_sin, sine_table, precision=highest)
    mixed_one = jnp.dot(sine_table * chirp_cos, cosines, precision=highest)
    mixed_two = jnp.dot(cosines * chirp_cos, sine_table, precision=highest)
    plain_one = jnp.dot(cosines * chirp_sin, cosines, precision=highest)
    plain_two = jnp.dot(sine_table * chirp_sin, sine_table, precision=highest)
    kernel_real = (cos_real + sin_real - sin_imag + cos_imag) / points
    kernel_imaginary = (mixed_one - mixed_two + plain_one + plain_two) / points
    propagator = (kernel_real.astype(jnp.bfloat16), kernel_imaginary.astype(jnp.bfloat16))
    return (fourier, propagator)

def complex_product(left_factor, right_factor):
    return (left_factor[0] * right_factor[0] - left_factor[1] * right_factor[1], left_factor[0] * right_factor[1] + left_factor[1] * right_factor[0])

def conjugate(operand):
    return (operand[0], -operand[1])

def to_half(operand):
    return (operand[0].astype(jnp.bfloat16), operand[1].astype(jnp.bfloat16))

def apply_left(matrix, operand):
    rows_count = matrix[0].shape[0]
    cols_count = operand[0].shape[1]
    stacked = jnp.concatenate([matrix[0], matrix[1]], axis=0)
    joined = jnp.concatenate([operand[0], operand[1]], axis=1)
    result = jnp.dot(stacked, joined, preferred_element_type=jnp.float32)
    return (result[:rows_count, :cols_count] - result[rows_count:, cols_count:], result[:rows_count, cols_count:] + result[rows_count:, :cols_count])

def apply_right(operand, matrix):
    rows_count = operand[0].shape[0]
    cols_count = matrix[0].shape[1]
    stacked = jnp.concatenate([operand[0], operand[1]], axis=0)
    joined = jnp.concatenate([matrix[0], matrix[1]], axis=1)
    result = jnp.dot(stacked, joined, preferred_element_type=jnp.float32)
    return (result[:rows_count, :cols_count] - result[rows_count:, cols_count:], result[:rows_count, cols_count:] + result[rows_count:, :cols_count])

def transform(matrix, operand):
    return apply_right(to_half(apply_left(matrix, operand)), matrix)

def slot_gradient(window, probe_field, measured, tables):
    fourier, propagator = tables
    layers = window.astype(jnp.float32)
    first_layer = (1.0 + layers[0, 0], layers[0, 1])
    second_layer = (1.0 + layers[1, 0], layers[1, 1])
    entrance = to_half(complex_product(probe_field, first_layer))
    middle = to_half(transform(propagator, entrance))
    middle_wide = (middle[0].astype(jnp.float32), middle[1].astype(jnp.float32))
    leaving = to_half(complex_product(middle_wide, second_layer))
    distant = transform(fourier, leaving)
    modulus = jnp.sqrt(distant[0] * distant[0] + distant[1] * distant[1] + smooth_floor)
    factor = 1.0 - measured.astype(jnp.float32) / modulus
    residual = to_half((factor * distant[0], factor * distant[1]))
    back_far = transform(conjugate(fourier), residual)
    back_middle = to_half(complex_product(back_far, conjugate(second_layer)))
    back_near = transform(conjugate(propagator), back_middle)
    first_grad = complex_product(back_near, conjugate(probe_field))
    second_grad = complex_product(back_far, conjugate(middle_wide))
    return jnp.stack([jnp.stack(first_grad), jnp.stack(second_grad)])

def window_at(source, corner, extent):
    anchor = jnp.zeros((), jnp.int32)
    return lax.dynamic_slice(source, (anchor, anchor, corner[0], corner[1]), (2, 2, extent, extent))

def add_window(accumulated, corner, update):
    extent = update.shape[-1]
    anchor = jnp.zeros((), jnp.int32)
    current = window_at(accumulated, corner, extent)
    return lax.dynamic_update_slice(accumulated, current + update, (anchor, anchor, corner[0], corner[1]))

def reference(object_field, probe_wave, positions, counts, amplitudes):
    probe_size = probe_wave.shape[1]
    half_width = probe_size // 2
    tables = make_tables(probe_size)
    probe_field = (probe_wave[0], probe_wave[1])
    slot_count = N_ROW * N_COL * P_MAX
    corners = positions.reshape(slot_count, 2).astype(jnp.int32)
    measured_all = amplitudes.reshape(slot_count, probe_size, probe_size)
    slot_numbers = jnp.arange(slot_count, dtype=jnp.int32)
    tile_index = slot_numbers // P_MAX
    active_slots = slot_numbers % P_MAX < counts.reshape(-1).astype(jnp.int32)[tile_index]
    offsets = jnp.stack([tile_index // N_COL * TILE, tile_index % N_COL * TILE], axis=1).astype(jnp.int32)
    global_corners = (corners + offsets).astype(jnp.int32)
    current = object_field
    for iteration in range(ITERS):
        padded = jnp.pad(current.astype(jnp.bfloat16), ((0, 0), (0, 0), (half_width, half_width), (half_width, half_width)))

        def compute(window, measured):
            return slot_gradient(window, probe_field, measured, tables)

        def nothing(window, measured):
            return jnp.zeros((2, 2, probe_size, probe_size), jnp.float32)

        def visit_slot(accumulated, element):
            corner, active, measured = element
            window = window_at(padded, corner, probe_size)
            update = lax.cond(active, compute, nothing, window, measured)
            return (add_window(accumulated, corner, update), None)
        gradient = lax.scan(visit_slot, jnp.zeros(padded.shape, jnp.float32), (global_corners, active_slots, measured_all))[0]
        current = current - descent_rate * gradient[:, :, half_width:half_width + NY, half_width:half_width + NX]
    return current
```

```python
import functools
import jax, jax.numpy as jnp
from jax import lax
import numpy as np
from jax.experimental import pallas as pl
from jax.experimental.pallas import tpu as pltpu
from jax.sharding import PartitionSpec as P

ITERS = 2
RATE = 0.1

N = 256
F32, BF16 = jnp.float32, jnp.bfloat16


def tables():
    k = np.arange(N)
    ang = 2 * np.pi * ((k[:, None] * k[None, :]) % N) / N
    f = np.exp(-1j * ang) / 16.0
    fk = np.where(k < N // 2, k, k - N).astype(np.float64)
    ker = (np.exp(-1j * np.pi * fk * fk / (2 * N))[None, :] * np.exp(1j * ang)).sum(1) / N
    p = ker[(k[:, None] - k[None, :]) % N]

    def block(m):
        return np.block([[m.real, -m.imag], [m.imag, m.real]]).astype(jnp.bfloat16)

    return np.stack([block(f), block(f.conj()), block(p), block(p.conj())])


def dot(a, b):
    return jnp.dot(a, b, preferred_element_type=F32)


def body(j, y, x, refs, LM, RM, RC):
    ext, grad, xs, yh, mid, sec, probe, amps, tab = refs
    q = x // 128
    s = x - q * 128
    back = (128 - s) % 128

    def lanes(rows):
        return lax.broadcasted_iota(jnp.int32, (rows, 128), 1)

    def window(p, r0, rows):
        parts = [pltpu.roll(ext[p, q + t, pl.ds(y + r0, rows), :], back, 1) for t in range(3)]
        keep = lanes(rows) < 128 - s
        return [jnp.where(keep, parts[t], parts[t + 1]) for t in range(2)]

    def cut(i, _):
        r0 = pl.multiple_of(i * RC, RC)
        wr, wi = window(0, r0, RC), window(1, r0, RC)
        sr, si = window(2, r0, RC), window(3, r0, RC)
        for t in range(2):
            cols = pl.ds(128 * t, 128)
            pr, pi = probe[0, pl.ds(r0, RC), cols], probe[1, pl.ds(r0, RC), cols]
            fr, fi = 1.0 + wr[t], wi[t]
            xs[pl.ds(r0, RC), cols] = (pr * fr - pi * fi).astype(BF16)
            xs[pl.ds(N + r0, RC), cols] = (pr * fi + pi * fr).astype(BF16)
            sec[0, pl.ds(r0, RC), cols] = 1.0 + sr[t]
            sec[1, pl.ds(r0, RC), cols] = si[t]
        return 0

    lax.fori_loop(0, N // RC, cut, 0, unroll=True)

    def left(m):
        for a in range(0, 2 * N, LM):
            out = dot(tab[m, a:a + LM, :], xs[...]).astype(BF16)
            if LM == 2 * N:
                yh[:, :N] = out[:N]
                yh[:, N:] = out[N:]
            else:
                yh[a % N:a % N + LM, (a // N) * N:(a // N) * N + N] = out

    def right(m, use):
        for a in range(0, N, RM):
            z = dot(yh[a:a + RM, :], tab[m, :, :])
            use(slice(a, a + RM), z[:, :N], z[:, N:])

    def put(rs, zr, zi):
        mr, mi = zr.astype(BF16), zi.astype(BF16)
        mid[0, rs, :] = mr
        mid[1, rs, :] = mi
        mr, mi = mr.astype(F32), mi.astype(F32)
        sr, si = sec[0, rs, :], sec[1, rs, :]
        xs[rs, :] = (mr * sr - mi * si).astype(BF16)
        xs[N + rs.start:N + rs.stop, :] = (mr * si + mi * sr).astype(BF16)

    left(2)
    right(3, put)

    def resid(rs, zr, zi):
        a = amps[j, rs, :].astype(F32)
        f = 1.0 - a * lax.rsqrt(zr * zr + zi * zi + 0.25)
        xs[rs, :] = (f * zr).astype(BF16)
        xs[N + rs.start:N + rs.stop, :] = (f * zi).astype(BF16)

    left(0)
    right(1, resid)

    def accumulate(p, rs, g):
        rows = rs.stop - rs.start
        g0, g1 = pltpu.roll(g[:, :128], s, 1), pltpu.roll(g[:, 128:], s, 1)
        hi = lanes(rows) >= s
        zero = jnp.zeros((rows, 128), F32)
        at = pl.ds(y + rs.start, rows)
        grad[p, q, at, :] += jnp.where(hi, g0, zero)
        grad[p, q + 1, at, :] += jnp.where(hi, g1, g0)
        grad[p, q + 2, at, :] += jnp.where(hi, zero, g1)

    def far(rs, zr, zi):
        mr, mi = mid[0, rs, :].astype(F32), mid[1, rs, :].astype(F32)
        accumulate(2, rs, zr * mr + zi * mi)
        accumulate(3, rs, zi * mr - zr * mi)
        sr, si = sec[0, rs, :], sec[1, rs, :]
        xs[rs, :] = (zr * sr + zi * si).astype(BF16)
        xs[N + rs.start:N + rs.stop, :] = (zi * sr - zr * si).astype(BF16)

    left(1)
    right(0, far)

    def near(rs, zr, zi):
        pr, pi = probe[0, rs, :], probe[1, rs, :]
        accumulate(0, rs, zr * pr + zi * pi)
        accumulate(1, rs, zi * pr - zr * pi)

    left(3)
    right(2, near)


def kernel(LM, RM, RC, cnt, pos, obj, hl, hr, hu, hd, probe, amps, tab, up, down, mids, ext, grad, xs, yh, mid, sec):
    for p in range(4):
        a, b = divmod(p, 2)
        for t in range(4):
            cols = slice(128 * t, 128 * t + 128)
            ext[p, t, 0:128, :] = hu[a, b, :, cols].astype(F32)
            ext[p, t, 384:512, :] = hd[a, b, :, cols].astype(F32)
        ext[p, 0, 128:384, :] = hl[a, b].astype(F32)
        ext[p, 3, 128:384, :] = hr[a, b].astype(F32)
        ext[p, 1, 128:384, :] = obj[a, b, :, 0:128].astype(BF16).astype(F32)
        ext[p, 2, 128:384, :] = obj[a, b, :, 128:256].astype(BF16).astype(F32)
    grad[...] = jnp.zeros(grad.shape, F32)
    refs = (ext, grad, xs, yh, mid, sec, probe, amps, tab)

    def step(j, _):
        body(j, pos[j, 0], pos[j, 1], refs, LM, RM, RC)
        return 0

    lax.fori_loop(0, cnt[0], step, 0)
    for p in range(4):
        a, b = divmod(p, 2)
        for t in range(4):
            cols = slice(128 * t, 128 * t + 128)
            up[a, b, :, cols] = grad[p, t, 0:128, :].astype(BF16)
            down[a, b, :, cols] = grad[p, t, 384:512, :].astype(BF16)
            mids[a, b, :, cols] = grad[p, t, 128:384, :]


def slots(cnt, pos, obj, hl, hr, hu, hd, probe, amps, tab, LM=256, RM=128, RC=32):
    V = pl.BlockSpec(memory_space=pltpu.VMEM)
    S = pl.BlockSpec(memory_space=pltpu.SMEM)
    return pl.pallas_call(
        functools.partial(kernel, LM, RM, RC),
        out_shape=(jax.ShapeDtypeStruct((2, 2, 128, 512), BF16), jax.ShapeDtypeStruct((2, 2, 128, 512), BF16),
                   jax.ShapeDtypeStruct((2, 2, 256, 512), F32)),
        in_specs=[S, S] + [V] * 8,
        out_specs=[V] * 3,
        scratch_shapes=[pltpu.VMEM((4, 5, 512, 128), F32), pltpu.VMEM((4, 5, 512, 128), F32),
                        pltpu.VMEM((512, 256), BF16), pltpu.VMEM((256, 512), BF16),
                        pltpu.VMEM((2, 256, 256), BF16), pltpu.VMEM((2, 256, 256), F32)],
        compiler_params=pltpu.CompilerParams(vmem_limit_bytes=48 << 20),
    )(cnt, pos, obj, hl, hr, hu, hd, probe, amps, tab)


def passed(value, axis, steps):
    count = lax.axis_size(axis)
    first, last = max(0, -steps), min(count, count - steps)
    return lax.ppermute(value, axis, [(i, i + steps) for i in range(first, last)])


def row_halos(band):
    return passed(band[:, :, 128:], "row", 1), passed(band[:, :, :128], "row", -1)


def shards(obj, probe, positions, counts, amplitudes):
    pos = positions.reshape(6, 2)
    cnt = counts.reshape(1)
    amps = amplitudes.reshape(6, N, N)
    tab = jnp.asarray(tables())
    column = lax.axis_index("col")
    half = obj.astype(BF16)
    hl = passed(half[..., 128:], "col", 1)
    hr = passed(half[..., :128], "col", -1)
    for it in range(ITERS):
        hu, hd = row_halos(jnp.concatenate([hl, obj.astype(BF16), hr], 3))
        up, down, mids = slots(cnt, pos, obj, hl, hr, hu, hd, probe, amps, tab)
        above, below = passed(down, "row", 1), passed(up, "row", -1)
        total = mids + jnp.concatenate([above, below], 2).astype(F32)
        if it + 1 < ITERS:
            right = passed(total[..., :256].astype(BF16), "col", -1).astype(F32)
            left = passed(total[..., 256:].astype(BF16), "col", 1).astype(F32)
            total = total + jnp.concatenate([left, right], 3)
            hl = jnp.where(column > 0, hl.astype(F32) - RATE * total[..., :128], 0.0).astype(BF16)
            hr = jnp.where(column + 1 < lax.axis_size("col"), hr.astype(F32) - RATE * total[..., 384:], 0.0).astype(BF16)
            obj = obj - RATE * total[..., 128:384]
        else:
            right = passed(total[..., :128].astype(BF16), "col", -1).astype(F32)
            left = passed(total[..., 384:].astype(BF16), "col", 1).astype(F32)
            obj = obj - RATE * (total[..., 128:384] + jnp.concatenate([left, right], 3))
    return obj


def solution(mesh):
    return jax.shard_map(
        shards,
        mesh=mesh,
        in_specs=(P(None, None, "row", "col"), P(), P("row", "col", None, None), P("row", "col"),
                  P("row", "col", None, None, None)),
        out_specs=P(None, None, "row", "col"),
        check_vma=False,
    )
```

```python
import functools
import jax, jax.numpy as jnp
from jax import lax
import numpy as np
from jax.experimental import pallas as pl
from jax.experimental.pallas import tpu as pltpu
from jax.sharding import PartitionSpec as P

RATE = 0.1
H = 128

N = 256
F32, BF16 = jnp.float32, jnp.bfloat16


def tables():
    k = np.arange(N)
    ang = 2 * np.pi * ((k[:, None] * k[None, :]) % N) / N
    f = np.exp(-1j * ang) / 16.0
    fk = np.where(k < N // 2, k, k - N).astype(np.float64)
    ker = (np.exp(-1j * np.pi * fk * fk / (2 * N))[None, :] * np.exp(1j * ang)).sum(1) / N
    p = ker[(k[:, None] - k[None, :]) % N]

    return np.stack([f.real, f.imag, p.real, p.imag]).astype(jnp.bfloat16)


def dot(a, b):
    return jnp.dot(a, b, preferred_element_type=F32)


def body(j, y, x, refs, LM, RM, RC):
    ext, grad, xs, yh, mid, sec, probe, amps, tab = refs
    q = x // 128
    s = x - q * 128
    back = (128 - s) % 128

    def lanes(rows):
        return lax.broadcasted_iota(jnp.int32, (rows, 128), 1)

    def window(p, r0, rows):
        parts = [pltpu.roll(ext[p, q + t, pl.ds(y + r0, rows), :], back, 1) for t in range(3)]
        keep = lanes(rows) < 128 - s
        return [jnp.where(keep, parts[t], parts[t + 1]) for t in range(2)]

    def cut(i, _):
        r0 = pl.multiple_of(i * RC, RC)
        wr, wi = window(0, r0, RC), window(1, r0, RC)
        sr, si = window(2, r0, RC), window(3, r0, RC)
        for t in range(2):
            cols = pl.ds(128 * t, 128)
            pr, pi = probe[0, pl.ds(r0, RC), cols], probe[1, pl.ds(r0, RC), cols]
            fr, fi = 1.0 + wr[t], wi[t]
            xs[pl.ds(r0, RC), cols] = (pr * fr - pi * fi).astype(BF16)
            xs[pl.ds(N + r0, RC), cols] = (pr * fi + pi * fr).astype(BF16)
            sec[0, pl.ds(r0, RC), cols] = 1.0 + sr[t]
            sec[1, pl.ds(r0, RC), cols] = si[t]
        return 0

    lax.fori_loop(0, N // RC, cut, 0, unroll=True)

    def left(m):
        for a in range(0, 2 * N, LM):
            out = dot(tab[m, a:a + LM, :], xs[...]).astype(BF16)
            if LM == 2 * N:
                yh[:, :N] = out[:N]
                yh[:, N:] = out[N:]
            else:
                yh[a % N:a % N + LM, (a // N) * N:(a // N) * N + N] = out

    def right(m, use):
        for a in range(0, N, RM):
            z = dot(yh[a:a + RM, :], tab[m, :, :])
            use(slice(a, a + RM), z[:, :N], z[:, N:])

    def put(rs, zr, zi):
        mr, mi = zr.astype(BF16), zi.astype(BF16)
        mid[0, rs, :] = mr
        mid[1, rs, :] = mi
        mr, mi = mr.astype(F32), mi.astype(F32)
        sr, si = sec[0, rs, :], sec[1, rs, :]
        xs[rs, :] = (mr * sr - mi * si).astype(BF16)
        xs[N + rs.start:N + rs.stop, :] = (mr * si + mi * sr).astype(BF16)

    left(2)
    right(3, put)

    def resid(rs, zr, zi):
        a = amps[j, rs, :].astype(F32)
        f = 1.0 - a * lax.rsqrt(zr * zr + zi * zi + 0.25)
        xs[rs, :] = (f * zr).astype(BF16)
        xs[N + rs.start:N + rs.stop, :] = (f * zi).astype(BF16)

    left(0)
    right(1, resid)

    def accumulate(p, rs, g):
        rows = rs.stop - rs.start
        g0, g1 = pltpu.roll(g[:, :128], s, 1), pltpu.roll(g[:, 128:], s, 1)
        hi = lanes(rows) >= s
        zero = jnp.zeros((rows, 128), F32)
        at = pl.ds(y + rs.start, rows)
        grad[p, q, at, :] += jnp.where(hi, g0, zero)
        grad[p, q + 1, at, :] += jnp.where(hi, g1, g0)
        grad[p, q + 2, at, :] += jnp.where(hi, zero, g1)

    def far(rs, zr, zi):
        mr, mi = mid[0, rs, :].astype(F32), mid[1, rs, :].astype(F32)
        accumulate(2, rs, zr * mr + zi * mi)
        accumulate(3, rs, zi * mr - zr * mi)
        sr, si = sec[0, rs, :], sec[1, rs, :]
        xs[rs, :] = (zr * sr + zi * si).astype(BF16)
        xs[N + rs.start:N + rs.stop, :] = (zi * sr - zr * si).astype(BF16)

    left(1)
    right(0, far)

    def near(rs, zr, zi):
        pr, pi = probe[0, rs, :], probe[1, rs, :]
        accumulate(0, rs, zr * pr + zi * pi)
        accumulate(1, rs, zi * pr - zr * pi)

    left(3)
    right(2, near)


PLANES = [(a, b) for a in range(2) for b in range(2)]
VM = pl.BlockSpec(memory_space=pltpu.VMEM)
SM = pl.BlockSpec(memory_space=pltpu.SMEM)


def local(fn, outs, specs, scratch=(), flops=0, moved=1 << 20, vmem=12 << 20):
    return pl.pallas_call(
        fn,
        out_shape=tuple(jax.ShapeDtypeStruct(s, d) for s, d in outs),
        in_specs=specs,
        out_specs=tuple(VM for _ in outs),
        scratch_shapes=list(scratch),
        cost_estimate=pl.CostEstimate(flops=flops, bytes_accessed=moved, transcendentals=0),
        compiler_params=pltpu.CompilerParams(vmem_limit_bytes=vmem),
    )


def parity():
    return lax.rem(lax.axis_index("row"), 2)


def block(k):
    return pl.multiple_of(jnp.where(parity() == 0, H * k, H * (3 - k)), H)


def own(k):
    return pl.multiple_of(jnp.where(parity() == k, 0, H), H)


def slots_kernel(LM, RM, RC, cnt, pos, ez, ec, hz, hc, probe, amps, tab, rz, rc, mz, mc,
                 ext, grad, xs, yh, mid, sec):
    for k, strip in enumerate((hz, ez, ec, hc)):
        at = pl.ds(block(k), H)
        for p, (a, b) in enumerate(PLANES):
            for t in range(4):
                ext[p, t, at, :] = strip[a, b, :, H * t:H * t + H].astype(F32)
    grad[...] = jnp.zeros(grad.shape, F32)
    refs = (ext, grad, xs, yh, mid, sec, probe, amps, tab)

    def step(j, _):
        body(j, pos[j, 0], pos[j, 1], refs, LM, RM, RC)
        return 0

    lax.fori_loop(0, cnt[0], step, 0)
    for k, strip in enumerate((rz, mz, mc, rc)):
        at = pl.ds(block(k), H)
        for p, (a, b) in enumerate(PLANES):
            for t in range(4):
                strip[a, b, :, H * t:H * t + H] = grad[p, t, at, :].astype(strip.dtype)


def slots(cnt, pos, ez, ec, hz, hc, probe, amps, tab, LM=256, RM=128, RC=32):
    s = (2, 2, H, 512)
    return local(
        functools.partial(slots_kernel, LM, RM, RC),
        [(s, BF16), (s, BF16), (s, F32), (s, F32)],
        [SM, SM] + [VM] * 7,
        [pltpu.VMEM((4, 5, 512, H), F32), pltpu.VMEM((4, 5, 512, H), F32),
         pltpu.VMEM((512, N), BF16), pltpu.VMEM((N, 512), BF16),
         pltpu.VMEM((2, N, N), BF16), pltpu.VMEM((2, N, N), F32)],
        flops=1 << 33, vmem=30 << 20,
    )(cnt, pos, ez, ec, hz, hc, probe, amps, tab)


def matrices_kernel(base, tab):
    for m in range(2):
        re, im = base[2 * m], base[2 * m + 1]
        for conj in range(2):
            k = 2 * m + conj
            tab[k, 0:N, 0:N] = re
            tab[k, N:, N:] = re
            tab[k, 0:N, N:] = im if conj else -im
            tab[k, N:, 0:N] = -im if conj else im


def edges_kernel(obj, lz, rz, lc, rc):
    for k, (left, right) in enumerate(((lz, rz), (lc, rc))):
        at = pl.ds(own(k), H)
        for a, b in PLANES:
            left[a, b] = obj[a, b, at, 0:H].astype(BF16)
            right[a, b] = obj[a, b, at, N - H:N].astype(BF16)


def join_kernel(k, obj, hl, hr, e):
    at = pl.ds(own(k), H)
    for a, b in PLANES:
        e[a, b, :, 0:H] = hl[a, b]
        e[a, b, :, H:3 * H] = obj[a, b, at, :].astype(BF16)
        e[a, b, :, 3 * H:] = hr[a, b]


def bands_kernel(width, m, rim, *outs):
    r0 = 0
    for i in range(0, len(outs), 2):
        rows = outs[i].shape[2]
        rs = slice(r0, r0 + rows)
        for a, b in PLANES:
            outs[i][a, b] = (m[a, b, rs, 0:width] + rim[a, b, rs, 0:width].astype(F32)).astype(BF16)
            outs[i + 1][a, b] = (m[a, b, rs, 512 - width:] + rim[a, b, rs, 512 - width:].astype(F32)).astype(BF16)
        r0 += rows


def update_kernel(k, chunks, m, rim, obj, e, *rest):
    arrived, (e_new, o_new) = rest[:2 * chunks], rest[2 * chunks:]
    column = lax.axis_index("col")
    keep_left = (column > 0).astype(F32)
    keep_right = (column < lax.axis_size("col") - 1).astype(F32)
    r0 = 0
    for i in range(chunks):
        from_left, from_right = arrived[2 * i], arrived[2 * i + 1]
        rows = from_left.shape[2]
        rs = slice(r0, r0 + rows)
        at = pl.ds(own(k) + r0, rows)
        for a, b in PLANES:
            for side, other, keep, c0 in ((0, from_left, keep_left, 0), (1, from_right, keep_right, N)):
                cols = slice(c0, c0 + N)
                total = RATE * (m[a, b, rs, cols] + rim[a, b, rs, cols].astype(F32) + other[a, b].astype(F32))
                outer = slice(0, H) if side == 0 else slice(H, N)
                inner = slice(H, N) if side == 0 else slice(0, H)
                halo = slice(0, H) if side == 0 else slice(3 * H, 4 * H)
                mine = slice(0, H) if side == 0 else slice(H, N)
                old = e[a, b, rs, halo].astype(F32)
                e_new[a, b, rs, halo] = (keep * (old - total[:, outer])).astype(BF16)
                value = obj[a, b, at, mine] - total[:, inner]
                o_new[a, b, rs, mine] = value
                e_new[a, b, rs, slice(H + mine.start, H + mine.stop)] = value.astype(BF16)
        r0 += rows


def finish_kernel(mz, rimz, oz, lz, rz, mc, rimc, oc, lc, rc, out):
    for k, (m, rim, o, left, right) in enumerate(((mz, rimz, oz, lz, rz), (mc, rimc, oc, lc, rc))):
        at = pl.ds(own(k), H)
        for a, b in PLANES:
            for side, other in ((0, left), (1, right)):
                cols = slice(H + H * side, 2 * H + H * side)
                mine = slice(H * side, H * side + H)
                total = m[a, b, :, cols] + rim[a, b, :, cols].astype(F32) + other[a, b].astype(F32)
                out[a, b, at, mine] = o[a, b, :, mine] - RATE * total


def moved(value, axis, steps):
    count = lax.axis_size(axis)
    first, last = max(0, -steps), min(count, count - steps)
    return lax.ppermute(value, axis, [(i, i + steps) for i in range(first, last)])


def swapped(value, first):
    count = lax.axis_size("row")
    pairs = [(i, i + 1) for i in range(first, count - 1, 2)]
    return lax.ppermute(value, "row", pairs + [(j, i) for i, j in pairs])


def sideways(left, right):
    return moved(right, "col", 1), moved(left, "col", -1)


def program(obj, probe, positions, counts, amplitudes):
    pos = positions.reshape(6, 2)
    cnt = counts.reshape(1)
    amps = amplitudes.reshape(6, N, N)
    strip, cut, band = (2, 2, H, 512), (2, 2, H, H), (2, 2, H, N)
    part = (2, 2, H // 2, N)

    lz, rz, lc, rc = local(edges_kernel, [(cut, BF16)] * 4, [VM])(obj)
    hl, hr = sideways(lz, rz)
    gl, gr = sideways(lc, rc)
    (ez,) = local(functools.partial(join_kernel, 0), [(strip, BF16)], [VM] * 3)(obj, hl, hr)
    hz = swapped(ez, 1)
    (ec,) = local(functools.partial(join_kernel, 1), [(strip, BF16)], [VM] * 3)(obj, gl, gr)
    hc = swapped(ec, 0)
    (tab,) = local(matrices_kernel, [((4, 2 * N, 2 * N), BF16)], [VM])(jnp.asarray(tables()))
    rim_z, rim_c, mz, mc = slots(cnt, pos, ez, ec, hz, hc, probe, amps, tab)

    in_c = swapped(rim_c, 0)
    in_z = swapped(rim_z, 1)
    l1, r1, l2, r2 = local(functools.partial(bands_kernel, N), [(part, BF16)] * 4, [VM] * 2)(mc, in_c)
    a1 = sideways(l1, r1)
    l0, r0 = local(functools.partial(bands_kernel, N), [(band, BF16)] * 2, [VM] * 2)(mz, in_z)
    a0 = sideways(l0, r0)
    a2 = sideways(l2, r2)
    half = (2, 2, H, N)
    ez2, oz = local(functools.partial(update_kernel, 0, 1), [(strip, BF16), (half, F32)], [VM] * 6)(
        mz, in_z, obj, ez, *a0)
    hz = swapped(ez2, 1)
    ec2, oc = local(functools.partial(update_kernel, 1, 2), [(strip, BF16), (half, F32)], [VM] * 8)(
        mc, in_c, obj, ec, *a1, *a2)
    hc = swapped(ec2, 0)
    rim_z, rim_c, mz, mc = slots(cnt, pos, ez2, ec2, hz, hc, probe, amps, tab)

    in_c = swapped(rim_c, 0)
    in_z = swapped(rim_z, 1)
    lc, rc = local(functools.partial(bands_kernel, H), [(cut, BF16)] * 2, [VM] * 2)(mc, in_c)
    ac = sideways(lc, rc)
    lz, rz = local(functools.partial(bands_kernel, H), [(cut, BF16)] * 2, [VM] * 2)(mz, in_z)
    az = sideways(lz, rz)
    (out,) = local(finish_kernel, [((2, 2, N, N), F32)], [VM] * 10)(
        mz, in_z, oz, *az, mc, in_c, oc, *ac)
    return out


def solution(mesh):
    return jax.shard_map(
        program,
        mesh=mesh,
        in_specs=(P(None, None, "row", "col"), P(), P("row", "col", None, None), P("row", "col"),
                  P("row", "col", None, None, None)),
        out_specs=P(None, None, "row", "col"),
        check_vma=False,
    )
```

```python
import functools
import jax, jax.numpy as jnp
from jax import lax
import numpy as np
from jax.experimental import pallas as pl
from jax.experimental.pallas import tpu as pltpu
from jax.sharding import PartitionSpec as P

RATE = 0.1
H = 128
FEW = 32

N = 256
F32, BF16 = jnp.float32, jnp.bfloat16


def tables():
    k = np.arange(N)
    ang = 2 * np.pi * ((k[:, None] * k[None, :]) % N) / N
    f = np.exp(-1j * ang) / 16.0
    fk = np.where(k < N // 2, k, k - N).astype(np.float64)
    ker = (np.exp(-1j * np.pi * fk * fk / (2 * N))[None, :] * np.exp(1j * ang)).sum(1) / N
    p = ker[(k[:, None] - k[None, :]) % N]

    return np.stack([f.real, f.imag, p.real, p.imag]).astype(jnp.bfloat16)


def dot(a, b):
    return jnp.dot(a, b, preferred_element_type=F32)


def body(j, y, x, refs, LM, RM, RC):
    ext, grad, xs, yh, mid, sec, probe, amps, tab = refs
    q = x // 128
    s = x - q * 128
    back = (128 - s) % 128

    def lanes(rows):
        return lax.broadcasted_iota(jnp.int32, (rows, 128), 1)

    def window(p, r0, rows):
        parts = [pltpu.roll(ext[p, q + t, pl.ds(y + r0, rows), :], back, 1) for t in range(3)]
        keep = lanes(rows) < 128 - s
        return [jnp.where(keep, parts[t], parts[t + 1]) for t in range(2)]

    def cut(i, _):
        r0 = pl.multiple_of(i * RC, RC)
        wr, wi = window(0, r0, RC), window(1, r0, RC)
        sr, si = window(2, r0, RC), window(3, r0, RC)
        for t in range(2):
            cols = pl.ds(128 * t, 128)
            pr, pi = probe[0, pl.ds(r0, RC), cols], probe[1, pl.ds(r0, RC), cols]
            fr, fi = 1.0 + wr[t], wi[t]
            xs[pl.ds(r0, RC), cols] = (pr * fr - pi * fi).astype(BF16)
            xs[pl.ds(N + r0, RC), cols] = (pr * fi + pi * fr).astype(BF16)
            sec[0, pl.ds(r0, RC), cols] = 1.0 + sr[t]
            sec[1, pl.ds(r0, RC), cols] = si[t]
        return 0

    lax.fori_loop(0, N // RC, cut, 0, unroll=True)

    def left(m):
        for a in range(0, 2 * N, LM):
            out = dot(tab[m, a:a + LM, :], xs[...]).astype(BF16)
            if LM == 2 * N:
                yh[:, :N] = out[:N]
                yh[:, N:] = out[N:]
            else:
                yh[a % N:a % N + LM, (a // N) * N:(a // N) * N + N] = out

    def right(m, use):
        for a in range(0, N, RM):
            z = dot(yh[a:a + RM, :], tab[m, :, :])
            use(slice(a, a + RM), z[:, :N], z[:, N:])

    def put(rs, zr, zi):
        mr, mi = zr.astype(BF16), zi.astype(BF16)
        mid[0, rs, :] = mr
        mid[1, rs, :] = mi
        mr, mi = mr.astype(F32), mi.astype(F32)
        sr, si = sec[0, rs, :], sec[1, rs, :]
        xs[rs, :] = (mr * sr - mi * si).astype(BF16)
        xs[N + rs.start:N + rs.stop, :] = (mr * si + mi * sr).astype(BF16)

    left(2)
    right(3, put)

    def resid(rs, zr, zi):
        a = amps[j, rs, :].astype(F32)
        f = 1.0 - a * lax.rsqrt(zr * zr + zi * zi + 0.25)
        xs[rs, :] = (f * zr).astype(BF16)
        xs[N + rs.start:N + rs.stop, :] = (f * zi).astype(BF16)

    left(0)
    right(1, resid)

    def accumulate(p, rs, g):
        rows = rs.stop - rs.start
        g0, g1 = pltpu.roll(g[:, :128], s, 1), pltpu.roll(g[:, 128:], s, 1)
        hi = lanes(rows) >= s
        zero = jnp.zeros((rows, 128), F32)
        at = pl.ds(y + rs.start, rows)
        grad[p, q, at, :] += jnp.where(hi, g0, zero)
        grad[p, q + 1, at, :] += jnp.where(hi, g1, g0)
        grad[p, q + 2, at, :] += jnp.where(hi, zero, g1)

    def far(rs, zr, zi):
        mr, mi = mid[0, rs, :].astype(F32), mid[1, rs, :].astype(F32)
        accumulate(2, rs, zr * mr + zi * mi)
        accumulate(3, rs, zi * mr - zr * mi)
        sr, si = sec[0, rs, :], sec[1, rs, :]
        xs[rs, :] = (zr * sr + zi * si).astype(BF16)
        xs[N + rs.start:N + rs.stop, :] = (zi * sr - zr * si).astype(BF16)

    left(1)
    right(0, far)

    def near(rs, zr, zi):
        pr, pi = probe[0, rs, :], probe[1, rs, :]
        accumulate(0, rs, zr * pr + zi * pi)
        accumulate(1, rs, zi * pr - zr * pi)

    left(3)
    right(2, near)


PLANES = [(a, b) for a in range(2) for b in range(2)]
VM = pl.BlockSpec(memory_space=pltpu.VMEM)
SM = pl.BlockSpec(memory_space=pltpu.SMEM)


def local(fn, outs, specs, scratch=(), places=None, flops=0, moved=1 << 20, vmem=8 << 20):
    return pl.pallas_call(
        fn,
        out_shape=tuple(jax.ShapeDtypeStruct(s, d) for s, d in outs),
        in_specs=specs,
        out_specs=tuple(places or [VM] * len(outs)),
        scratch_shapes=list(scratch),
        cost_estimate=pl.CostEstimate(flops=flops, bytes_accessed=moved, transcendentals=0),
        compiler_params=pltpu.CompilerParams(vmem_limit_bytes=vmem),
    )


def parity():
    return lax.rem(lax.axis_index("row"), 2)


def block(k):
    return pl.multiple_of(jnp.where(parity() == 0, H * k, H * (3 - k)), H)


def own(k):
    return pl.multiple_of(jnp.where(parity() == k, 0, H), H)


def slots_kernel(LM, RM, RC, scalars, ez, ec, hz, hc, probe, amps, base, rz, rc, mz, mc,
                 ext, grad, xs, yh, mid, sec, tab):
    for m in range(2):
        re, im = base[2 * m], base[2 * m + 1]
        for conj in range(2):
            k = 2 * m + conj
            tab[k, 0:N, 0:N] = re
            tab[k, N:, N:] = re
            tab[k, 0:N, N:] = im if conj else -im
            tab[k, N:, 0:N] = -im if conj else im
    for k, strip in enumerate((hz, ez, ec, hc)):
        at = pl.ds(block(k), H)
        for p, (a, b) in enumerate(PLANES):
            for t in range(4):
                ext[p, t, at, :] = strip[a, b, :, H * t:H * t + H].astype(F32)
    grad[...] = jnp.zeros(grad.shape, F32)
    refs = (ext, grad, xs, yh, mid, sec, probe, amps, tab)

    def step(j, _):
        body(j, scalars[2 * j + 1], scalars[2 * j + 2], refs, LM, RM, RC)
        return 0

    lax.fori_loop(0, scalars[0], step, 0)
    for k, strip in enumerate((rz, mz, mc, rc)):
        at = pl.ds(block(k), H)
        for p, (a, b) in enumerate(PLANES):
            for t in range(4):
                strip[a, b, :, H * t:H * t + H] = grad[p, t, at, :].astype(strip.dtype)


def slots(scalars, ez, ec, hz, hc, probe, amps, base, LM=256, RM=128, RC=32):
    s = (2, 2, H, 512)
    return local(
        functools.partial(slots_kernel, LM, RM, RC),
        [(s, BF16), (s, BF16), (s, F32), (s, F32)],
        [SM] + [VM] * 7,
        [pltpu.VMEM((4, 5, 512, H), F32), pltpu.VMEM((4, 5, 512, H), F32),
         pltpu.VMEM((512, N), BF16), pltpu.VMEM((N, 512), BF16),
         pltpu.VMEM((2, N, N), BF16), pltpu.VMEM((2, N, N), F32),
         pltpu.VMEM((4, 2 * N, 2 * N), BF16)],
        flops=1 << 33, vmem=20 << 20,
    )(scalars, ez, ec, hz, hc, probe, amps, base)


def by_column(run, inner, outer):
    odd = lax.rem(lax.axis_index("col"), 2)
    pl.when(odd == 0)(lambda: run(outer, inner))
    pl.when(odd == 1)(lambda: run(inner, outer))


def setup_kernel(base, pos, cnt, kept, scalars):
    kept[...] = base[...]
    scalars[0] = cnt[0, 0]
    for j in range(6):
        scalars[2 * j + 1] = pos[0, 0, j, 0]
        scalars[2 * j + 2] = pos[0, 0, j, 1]


def edges_kernel(obj, iz, oz, ic, oc):
    def run(left, right):
        for k in range(2):
            at = pl.ds(own(k), H)
            for a, b in PLANES:
                left[k][a, b] = obj[a, b, at, 0:H].astype(BF16)
                right[k][a, b] = obj[a, b, at, N - H:N].astype(BF16)

    by_column(run, (iz, ic), (oz, oc))


def join_kernel(k, obj, inner, outer, e):
    at = pl.ds(own(k), H)

    def run(left, right):
        for a, b in PLANES:
            e[a, b, :, 0:H] = left[a, b]
            e[a, b, :, H:3 * H] = obj[a, b, at, :].astype(BF16)
            e[a, b, :, 3 * H:] = right[a, b]

    by_column(run, inner, outer)


def bands_kernel(width, m, rim, *outs):
    def run(left, right):
        r0 = 0
        for l, r in zip(left, right):
            rs = slice(r0, r0 + l.shape[2])
            for a, b in PLANES:
                l[a, b] = (m[a, b, rs, 0:width] + rim[a, b, rs, 0:width].astype(F32)).astype(BF16)
                r[a, b] = (m[a, b, rs, 512 - width:] + rim[a, b, rs, 512 - width:].astype(F32)).astype(BF16)
            r0 = rs.stop

    by_column(run, outs[0::2], outs[1::2])


def update_kernel(k, chunks, m, rim, obj, e, *rest):
    arrived, (e_new, o_new) = rest[:2 * chunks], rest[2 * chunks:]
    column = lax.axis_index("col")
    keep_left = (column > 0).astype(F32)
    keep_right = (column < lax.axis_size("col") - 1).astype(F32)

    def run(lefts, rights):
        r0 = 0
        for from_left, from_right in zip(lefts, rights):
            rows = from_left.shape[2]
            rs = slice(r0, r0 + rows)
            at = pl.ds(own(k) + r0, rows)
            for a, b in PLANES:
                for side, other, keep in ((0, from_left, keep_left), (1, from_right, keep_right)):
                    cols = slice(N * side, N * side + N)
                    total = RATE * (m[a, b, rs, cols] + rim[a, b, rs, cols].astype(F32) + other[a, b].astype(F32))
                    outside, inside = (slice(0, H), slice(H, N)) if side == 0 else (slice(H, N), slice(0, H))
                    halo = slice(3 * H * side, 3 * H * side + H)
                    mine = slice(H * side, H * side + H)
                    old = e[a, b, rs, halo].astype(F32)
                    e_new[a, b, rs, halo] = (keep * (old - total[:, outside])).astype(BF16)
                    value = obj[a, b, at, mine] - total[:, inside]
                    o_new[a, b, rs, mine] = value
                    e_new[a, b, rs, slice(H + mine.start, H + mine.stop)] = value.astype(BF16)
            r0 += rows

    by_column(run, arrived[0::2], arrived[1::2])


def finish_kernel(mz, rimz, oz, inz, outz, mc, rimc, oc, inc, outc, out):
    def run(left, right):
        for k, (m, rim, o) in enumerate(((mz, rimz, oz), (mc, rimc, oc))):
            at = pl.ds(own(k), H)
            for a, b in PLANES:
                for side, other in ((0, left[k]), (1, right[k])):
                    cols = slice(H + H * side, 2 * H + H * side)
                    mine = slice(H * side, H * side + H)
                    total = m[a, b, :, cols] + rim[a, b, :, cols].astype(F32) + other[a, b].astype(F32)
                    out[a, b, at, mine] = o[a, b, :, mine] - RATE * total

    by_column(run, (inz, inc), (outz, outc))


def swapped(value, axis, first):
    pairs = [(i, i + 1) for i in range(first, lax.axis_size(axis) - 1, 2)]
    return lax.ppermute(value, axis, pairs + [(j, i) for i, j in pairs])


def sideways(inner, outer):
    return swapped(inner, "col", 0), swapped(outer, "col", 1)


def program(obj, probe, positions, counts, amplitudes):
    amps = amplitudes.reshape(6, N, N)
    strip, cut, band, half = (2, 2, H, 512), (2, 2, H, H), (2, 2, H, N), (2, 2, H, N)
    few, rest = (2, 2, FEW, N), (2, 2, H - FEW, N)

    iz, oz, ic, oc = local(edges_kernel, [(cut, BF16)] * 4, [VM])(obj)
    hi, ho = sideways(iz, oz)
    gi, go = sideways(ic, oc)
    base, scalars = local(setup_kernel, [((4, N, N), BF16), ((13,), jnp.int32)], [VM, SM, SM],
                          places=[VM, SM])(jnp.asarray(tables()), positions, counts)
    (ez,) = local(functools.partial(join_kernel, 0), [(strip, BF16)], [VM] * 3)(obj, hi, ho)
    hz = swapped(ez, "row", 1)
    (ec,) = local(functools.partial(join_kernel, 1), [(strip, BF16)], [VM] * 3)(obj, gi, go)
    hc = swapped(ec, "row", 0)
    rim_z, rim_c, mz, mc = slots(scalars, ez, ec, hz, hc, probe, amps, base)

    in_c = swapped(rim_c, "row", 0)
    in_z = swapped(rim_z, "row", 1)
    i1, o1, i2, o2 = local(functools.partial(bands_kernel, N), [(few, BF16)] * 2 + [(rest, BF16)] * 2, [VM] * 2)(mc, in_c)
    a1 = sideways(i1, o1)
    i0, o0 = local(functools.partial(bands_kernel, N), [(band, BF16)] * 2, [VM] * 2)(mz, in_z)
    a0 = sideways(i0, o0)
    a2 = sideways(i2, o2)
    ez2, oz = local(functools.partial(update_kernel, 0, 1), [(strip, BF16), (half, F32)], [VM] * 6)(
        mz, in_z, obj, ez, *a0)
    hz = swapped(ez2, "row", 1)
    ec2, oc = local(functools.partial(update_kernel, 1, 2), [(strip, BF16), (half, F32)], [VM] * 8)(
        mc, in_c, obj, ec, *a1, *a2)
    hc = swapped(ec2, "row", 0)
    rim_z, rim_c, mz, mc = slots(scalars, ez2, ec2, hz, hc, probe, amps, base)

    in_c = swapped(rim_c, "row", 0)
    in_z = swapped(rim_z, "row", 1)
    ic, oc_ = local(functools.partial(bands_kernel, H), [(cut, BF16)] * 2, [VM] * 2)(mc, in_c)
    ac = sideways(ic, oc_)
    iz, oz_ = local(functools.partial(bands_kernel, H), [(cut, BF16)] * 2, [VM] * 2)(mz, in_z)
    az = sideways(iz, oz_)
    (out,) = local(finish_kernel, [((2, 2, N, N), F32)], [VM] * 10)(
        mz, in_z, oz, *az, mc, in_c, oc, *ac)
    return out


def solution(mesh):
    return jax.shard_map(
        program,
        mesh=mesh,
        in_specs=(P(None, None, "row", "col"), P(), P("row", "col", None, None), P("row", "col"),
                  P("row", "col", None, None, None)),
        out_specs=P(None, None, "row", "col"),
        check_vma=False,
    )
```
